128 devices in a mesh: dp: 16 (over y, z_lo, core), freq: 8 (over x, z_hi).
Axes of the slice: x: 4, y: 4, z: 4 (z_hi: 2, z_lo: 2; z = z_hi * 2 + z_lo), core: 2. Of those that a mesh axis runs over, the one named last changes fastest.
Arguments:
- records: float32 [16, 2, 1024, 2048], P('dp', None, None, 'freq'), may hold values from -6 to 6
- stem_weight: bfloat16 [256, 512], replicated, may hold values from -0.375 to 0.375
- conv_weight: bfloat16 [3, 3, 16, 512], replicated, may hold values from -0.875 to 0.875
- mix_weight: bfloat16 [3, 512, 512], replicated, may hold values from -0.25 to 0.25
- head_weight: float32 [512, 10], replicated, may hold values from -0.25 to 0.25
- labels: int32 [16], P('dp'), may hold values from 0 to 9
- band_bounds: int32 [33], replicated, may hold values from 0 to 1048576, as said below
Outputs:
- loss: float32 [], replicated
- grad_stem: float32 [256, 512], replicated
- grad_conv: float32 [3, 3, 16, 512], replicated
- grad_mix: float32 [3, 512, 512], replicated
- grad_head: float32 [512, 10], replicated
The draws below stay inside these ranges and needn't reach their ends.
Inputs may be any that keep to these rules, and one draw needn't show every extreme that they name: `band_bounds`: strictly increasing multiples of 128; the first is 0 and the last is half of 2097152.
All inputs are finite; a program needn't handle non-finite values.
Results may differ from the reference program's by a relative error of at most 0.0018.
Values may be sent and summed in bfloat16 or wider, within the bound.
A program may use at most 128 MiB of HBM per device.

```python
import jax
import jax.numpy as jnp
from jax import lax

RECORDS = 16
N1 = 1024
N2 = 2048
POOL = 128
CHANNELS = 512
GROUP_WIDTH = 16
KW = 3
LAYERS = 3
CLASSES = 10


def draw_band_bounds(key, part):
    positions = N1 * N2 // 2 // POOL
    bands = CHANNELS // GROUP_WIDTH
    cuts = jax.random.permutation(key, positions - 1)[:bands - 1] + 1
    cuts = jnp.sort(cuts).astype(jnp.int32)
    edges = jnp.concatenate([jnp.zeros((1,), jnp.int32), cuts, jnp.full((1,), positions, jnp.int32)])
    return (edges * POOL).astype(jnp.int32)


def with_ends(values, key, low, top_value):
    longest = values.shape.index(max(values.shape))
    spots = []
    for shift in (0, 1):
        where = [jax.random.randint(jax.random.fold_in(key, axis), (), 0, length) for axis, length in enumerate(values.shape)]
        where[longest] = (where[longest] + shift) % values.shape[longest]
        spots.append(tuple(where))
    return values.at[spots[0]].set(low).at[spots[1]].set(top_value)


def shard_levels(key, dims, split, least, top_value):
    level, own = 1.0, jax.random.fold_in(key, 6)
    for axis_at, shards_of in split:
        steps = jnp.exp(jax.random.uniform(jax.random.fold_in(own, axis_at), (shards_of,), jnp.float32, least / len(split), top_value / len(split)))
        level = level * jnp.repeat(steps, dims[axis_at] // shards_of).reshape([-1 if axis == axis_at else 1 for axis in range(len(dims))])
    return level


def centred(key, extent, scale, limit, shards=(), kind=jnp.bfloat16):
    loudness = shard_levels(key, extent, shards, -0.22, 0.18) if shards else 1.0
    drawn = jax.random.normal(key, extent, jnp.float32) * scale * loudness
    return jnp.minimum(jnp.maximum(drawn, -limit), limit).astype(kind)


def setup_inputs(seed: int = 0) -> dict:
    key_list = jax.random.split(jax.random.key(seed), 8)
    records = centred(key_list[0], (RECORDS, 2, N1, N2), 1.0, 6.0, ((0, 16), (3, 8)), jnp.float32)
    stem_weight = centred(key_list[1], (2 * POOL, CHANNELS), (2 * POOL) ** -0.5, 0.375)
    conv_weight = centred(key_list[2], (LAYERS, KW, GROUP_WIDTH, CHANNELS), (KW * GROUP_WIDTH) ** -0.5, 0.875)
    mix_weight = centred(key_list[3], (LAYERS, CHANNELS, CHANNELS), CHANNELS ** -0.5, 0.25)
    head_weight = centred(key_list[4], (CHANNELS, CLASSES), CHANNELS ** -0.5, 0.25, (), jnp.float32)
    labels = with_ends(jax.random.randint(key_list[5], (RECORDS,), 0, CLASSES), jax.random.fold_in(key_list[5], 1), 0, CLASSES - 1).astype(jnp.int32)
    band_bounds = draw_band_bounds(jax.random.fold_in(key_list[7], 71), 0)
    return {"records": records, "stem_weight": stem_weight, "conv_weight": conv_weight, "mix_weight": mix_weight, "head_weight": head_weight, "labels": labels, "band_bounds": band_bounds}


EXACT_DOTS = lax.Precision.HIGHEST
EPS = 1e-05

def spectra_features(record):
    total_len = N1 * N2
    signal = (record[0] + 1j * record[1]).reshape(total_len)
    angles = jnp.arange(total_len).astype(record.dtype) * (jnp.pi / total_len)
    signal = signal * (jnp.cos(angles) - 1j * jnp.sin(angles))
    spectrum = jnp.fft.fft(signal)
    mirrored = spectrum[::-1]
    z_real = jnp.real(spectrum)
    z_imag = jnp.imag(spectrum)
    m_real = jnp.real(mirrored)
    m_imag = jnp.imag(mirrored)
    half_len = total_len // 2
    power_a = (((z_real + m_real) ** 2 + (z_imag - m_imag) ** 2) * 0.25)[:half_len]
    power_b = (((z_imag + m_imag) ** 2 + (z_real - m_real) ** 2) * 0.25)[:half_len]
    feat_a = jnp.log1p(power_a / total_len).reshape(half_len // POOL, POOL)
    feat_b = jnp.log1p(power_b / total_len).reshape(half_len // POOL, POOL)
    return jnp.concatenate([feat_a, feat_b], axis=1).astype(jnp.bfloat16)

def conv_forward(padded, tap_weights, span_len):
    groups = padded.shape[-1] // GROUP_WIDTH
    record_count = padded.shape[0]
    result = jnp.zeros((record_count, span_len, groups, GROUP_WIDTH), jnp.float32)
    for tap_idx in range(KW):
        window = padded[:, tap_idx:tap_idx + span_len].astype(jnp.float32).reshape(record_count, span_len, groups, GROUP_WIDTH)
        kernel = tap_weights[tap_idx].astype(jnp.float32).reshape(GROUP_WIDTH, groups, GROUP_WIDTH)
        result = result + jnp.einsum('rpgi,igo->rpgo', window, kernel, precision=EXACT_DOTS)
    return result.reshape(record_count, span_len, groups * GROUP_WIDTH)

def conv_backward(grad_padded, tap_weights, span_len):
    groups = grad_padded.shape[-1] // GROUP_WIDTH
    record_count = grad_padded.shape[0]
    result = jnp.zeros((record_count, span_len, groups, GROUP_WIDTH), jnp.float32)
    for tap_idx in range(KW):
        shift_at = KW - 1 - tap_idx
        window = grad_padded[:, shift_at:shift_at + span_len].astype(jnp.float32).reshape(record_count, span_len, groups, GROUP_WIDTH)
        kernel = tap_weights[tap_idx].astype(jnp.float32).reshape(GROUP_WIDTH, groups, GROUP_WIDTH)
        result = result + jnp.einsum('rpgo,igo->rpgi', window, kernel, precision=EXACT_DOTS)
    return result.reshape(record_count, span_len, groups * GROUP_WIDTH)

def conv_weight_grad(padded, grad_pre, span_len):
    groups = padded.shape[-1] // GROUP_WIDTH
    record_count = padded.shape[0]
    grad_split = grad_pre.astype(jnp.float32).reshape(record_count, span_len, groups, GROUP_WIDTH)
    tap_list = []
    for tap_idx in range(KW):
        window = padded[:, tap_idx:tap_idx + span_len].astype(jnp.float32).reshape(record_count, span_len, groups, GROUP_WIDTH)
        tap_grad = jnp.einsum('rpgi,rpgo->igo', window, grad_split, precision=EXACT_DOTS)
        tap_list.append(tap_grad.reshape(GROUP_WIDTH, groups * GROUP_WIDTH))
    return jnp.stack(tap_list)

def record_step(record, label, stem_weight, conv_weight, mix_weight, head_weight, band_bounds):
    features_in = spectra_features(record)[None]
    positions = features_in.shape[1]
    channels = stem_weight.shape[1]
    groups = channels // GROUP_WIDTH
    stream = jnp.einsum('rpf,fc->rpc', features_in.astype(jnp.float32), stem_weight.astype(jnp.float32), precision=EXACT_DOTS)
    saved_layers = []
    for layer_idx in range(LAYERS):
        scales = lax.rsqrt(lax.optimization_barrier(jnp.mean(stream * stream, axis=-1, keepdims=True)) + EPS)
        normed = (stream * scales).astype(jnp.bfloat16)
        padded = jnp.pad(normed, ((0, 0), (1, 1), (0, 0)))
        preact = conv_forward(padded, conv_weight[layer_idx], positions)
        activated = jax.nn.silu(preact).astype(jnp.bfloat16)
        saved_layers.append((stream, padded, preact, activated))
        stream = stream + jnp.einsum('rpc,cd->rpd', activated.astype(jnp.float32), mix_weight[layer_idx].astype(jnp.float32), precision=EXACT_DOTS)
    starts = (jnp.arange(positions) * POOL).astype(jnp.int32)[:, None]
    member = ((starts >= band_bounds[None, :-1]) & (starts < band_bounds[None, 1:])).astype(jnp.float32)
    counts = ((band_bounds[1:] - band_bounds[:-1]) // POOL).astype(jnp.float32)
    band_sum = jnp.einsum('pg,rpgo->rgo', member, stream.reshape(1, positions, groups, GROUP_WIDTH), precision=EXACT_DOTS)
    pooled = (band_sum / counts[:, None]).reshape(1, channels)
    logits = jnp.dot(pooled, head_weight, precision=EXACT_DOTS)
    exponents = jnp.exp(logits)
    denominator = lax.optimization_barrier(jnp.sum(exponents, axis=-1, keepdims=True))
    one_hot = (jnp.arange(CLASSES) == label).astype(jnp.float32)[None]
    loss_term = jnp.sum(jnp.log(denominator[:, 0]) - lax.optimization_barrier(jnp.sum(one_hot * logits, axis=-1))) / RECORDS
    grad_logits = (exponents / denominator - one_hot) / RECORDS
    grad_head = jnp.dot(pooled.T, grad_logits, precision=EXACT_DOTS)
    grad_band = jnp.dot(grad_logits, head_weight.T, precision=EXACT_DOTS).reshape(1, groups, GROUP_WIDTH) / counts[:, None]
    grad_stream = (member[None, :, :, None] * grad_band[:, None]).reshape(1, positions, channels)
    conv_grads = [None] * LAYERS
    mix_grads = [None] * LAYERS
    for layer_idx in reversed(range(LAYERS)):
        stream_in, padded, preact, activated = saved_layers[layer_idx]
        grad_out = grad_stream.astype(jnp.bfloat16)
        mix_grads[layer_idx] = jnp.einsum('rpc,rpd->cd', activated.astype(jnp.float32), grad_out.astype(jnp.float32), precision=EXACT_DOTS)
        grad_act = jnp.einsum('rpd,cd->rpc', grad_out.astype(jnp.float32), mix_weight[layer_idx].astype(jnp.float32), precision=EXACT_DOTS)
        gate_value = jax.nn.sigmoid(preact)
        grad_pre = (grad_act * gate_value * (1.0 + preact * (1.0 - gate_value))).astype(jnp.bfloat16)
        grad_padded = jnp.pad(grad_pre, ((0, 0), (1, 1), (0, 0)))
        grad_normed = conv_backward(grad_padded, conv_weight[layer_idx], positions)
        conv_grads[layer_idx] = conv_weight_grad(padded, grad_pre, positions)
        scales = lax.rsqrt(lax.optimization_barrier(jnp.mean(stream_in * stream_in, axis=-1, keepdims=True)) + EPS)
        grad_stream = grad_stream + scales * grad_normed - stream_in * scales ** 3 * lax.optimization_barrier(jnp.mean(stream_in * grad_normed, axis=-1, keepdims=True))
    grad_stem = jnp.einsum('rpf,rpc->fc', features_in.astype(jnp.float32), grad_stream, precision=EXACT_DOTS)
    return (loss_term, grad_stem, jnp.stack(conv_grads), jnp.stack(mix_grads), grad_head)

def reference(records, stem_weight, conv_weight, mix_weight, head_weight, labels, band_bounds):

    def one_record(paired):
        return record_step(paired[0], paired[1], stem_weight, conv_weight, mix_weight, head_weight, band_bounds)
    results = lax.map(one_record, (records, labels))
    return (jnp.sum(results[0]), lax.optimization_barrier(jnp.sum(results[1], axis=0)), lax.optimization_barrier(jnp.sum(results[2], axis=0)), lax.optimization_barrier(jnp.sum(results[3], axis=0)), lax.optimization_barrier(jnp.sum(results[4], axis=0)))
```

```python
import functools

import jax
import jax.numpy as jnp
import numpy as np
from jax import lax
from jax.experimental import pallas as pl
from jax.experimental.pallas import tpu as pltpu
from jax.sharding import PartitionSpec as P

EXACT_DOTS = lax.Precision.HIGHEST
EPS = 1e-05
N1 = 1024
N2 = 2048
TOTAL = N1 * N2
POOL = 128
GROUP_WIDTH = 16
KW = 3
PARTS = 8
COLS = N2 // PARTS
HALO = 8
BLOCK_ROWS = N2 // 2 // PARTS + 2 * HALO
BF16 = jnp.bfloat16
F32 = jnp.float32


def split_host(values):
    high = np.asarray(values, np.float32).astype(jnp.bfloat16)
    low = (values - high.astype(np.float64)).astype(jnp.bfloat16)
    return high, low


def first_tables():
    rows = np.arange(N1 // 2, dtype=np.int64)[:, None]
    samples = np.arange(N1 // 2, dtype=np.int64)[None]
    angles = -np.pi * (samples * (2 * rows + 1) % (2 * N1)) / N1
    blocks = [np.cos(angles).reshape(4, 128, -1), np.sin(angles).reshape(4, 128, -1)]
    return split_host(np.stack(blocks, axis=1).reshape(4 * 256, N1 // 2))


def turn_tables():
    rows = np.arange(N1 // 2, dtype=np.int64)[:, None]
    columns = np.arange(COLS, dtype=np.int64)[None]
    angles = -np.pi * (columns * (2 * rows + 1)) / TOTAL
    device_angles = -np.pi * (COLS * np.arange(PARTS, dtype=np.int64)[None] * (2 * rows + 1)) / TOTAL
    shared = np.stack([np.cos(angles), np.sin(angles)]).astype(np.float32)
    own = np.concatenate([np.cos(device_angles), np.sin(device_angles)], axis=1).astype(np.float32)
    return shared, own


def second_tables():
    order = np.concatenate([np.arange(128), np.arange(255, 127, -1)]).astype(np.int64)
    columns = np.arange(COLS, dtype=np.int64)[None]
    angles = -2 * np.pi * (order[:, None] * columns % COLS) / COLS
    cosine, sine = np.cos(angles), np.sin(angles)
    upper = np.concatenate([cosine, -sine], axis=1)
    lower = np.concatenate([sine, cosine], axis=1)
    lanes = -2 * np.pi * (np.arange(PARTS, dtype=np.int64)[:, None] * columns) / N2
    turn = np.concatenate([np.cos(lanes), np.sin(lanes)], axis=0).astype(np.float32)
    return split_host(np.concatenate([upper, lower], axis=0)) + (turn,)


def three_pass(lhs_high, lhs_low, rhs_high, rhs_low, dims):
    product = functools.partial(
        lax.dot_general, dimension_numbers=(dims, ((), ())), preferred_element_type=F32
    )
    return product(lhs_high, rhs_high) + (product(lhs_high, rhs_low) + product(lhs_low, rhs_high))


def first_kernel(x_ref, th_ref, tl_ref, turn_ref, own_ref, out_ref, xh_ref, xl_ref):
    @pl.when(pl.program_id(0) == 0)
    def _():
        for channel in range(2):
            for piece in range(4):
                rows = pl.ds(piece * 256, 256)
                value = x_ref[channel, rows, :]
                high = value.astype(BF16)
                xh_ref[channel, rows, :] = high
                xl_ref[channel, rows, :] = (value - high.astype(F32)).astype(BF16)

    place = lax.axis_index("freq")
    lane = lax.broadcasted_iota(jnp.int32, (128, 2 * PARTS), 1)
    own = own_ref[...]
    own_cos = jnp.sum(jnp.where(lane == place, own, 0.0), axis=1, keepdims=True)
    own_sin = jnp.sum(jnp.where(lane == place + PARTS, own, 0.0), axis=1, keepdims=True)
    cosine = turn_ref[0] * own_cos - turn_ref[1] * own_sin
    sine = turn_ref[0] * own_sin + turn_ref[1] * own_cos
    row = lax.broadcasted_iota(jnp.int32, (128, COLS), 0)
    sign = jnp.where(row % 2 == 0, 1.0, -1.0)
    for channel in range(2):
        parts = []
        for half in range(2):
            rows = pl.ds(half * 512, 512)
            parts.append(
                three_pass(
                    th_ref[...], tl_ref[...], xh_ref[channel, rows, :], xl_ref[channel, rows, :],
                    ((1,), (0,)),
                )
            )
        real = parts[0][:128] + sign * parts[1][128:]
        imag = parts[0][128:] - sign * parts[1][:128]
        out_ref[channel, 0] = (real * cosine - imag * sine).astype(BF16)
        out_ref[channel, 1] = (real * sine + imag * cosine).astype(BF16)


def first_section(records):
    table_high, table_low = first_tables()
    shared, own = turn_tables()
    return pl.pallas_call(
        first_kernel,
        grid=(4,),
        out_shape=jax.ShapeDtypeStruct((PARTS, 2, 128, COLS), BF16),
        in_specs=[
            pl.BlockSpec((2, N1, COLS), lambda j: (0, 0, 0)),
            pl.BlockSpec((256, 512), lambda j: (j, 0)),
            pl.BlockSpec((256, 512), lambda j: (j, 0)),
            pl.BlockSpec((2, 128, COLS), lambda j: (0, j, 0)),
            pl.BlockSpec((128, 2 * PARTS), lambda j: (j, 0)),
        ],
        out_specs=pl.BlockSpec((2, 2, 128, COLS), lambda j: (j, 0, 0, 0)),
        scratch_shapes=[pltpu.VMEM((2, N1, COLS), BF16)] * 2,
        name="first_section",
    )(records, jnp.asarray(table_high), jnp.asarray(table_low), jnp.asarray(shared), jnp.asarray(own))


def eight_point(values):
    root = np.float32(np.sqrt(0.5))

    def add(a, b):
        return (a[0] + b[0], a[1] + b[1])

    def sub(a, b):
        return (a[0] - b[0], a[1] - b[1])

    def quarter(a):
        return (a[1], -a[0])

    def four(a):
        s02, d02, s13, d13 = add(a[0], a[2]), sub(a[0], a[2]), add(a[1], a[3]), sub(a[1], a[3])
        turned = quarter(d13)
        return [add(s02, s13), add(d02, turned), sub(s02, s13), sub(d02, turned)]

    even, odd = four(values[0::2]), four(values[1::2])
    turned = [
        odd[0],
        ((odd[1][0] + odd[1][1]) * root, (odd[1][1] - odd[1][0]) * root),
        quarter(odd[2]),
        ((odd[3][1] - odd[3][0]) * root, -(odd[3][0] + odd[3][1]) * root),
    ]
    return [add(even[i], turned[i]) for i in range(4)] + [sub(even[i], turned[i]) for i in range(4)]


def combine_columns(load, turn_ref, wh_ref, wl_ref):
    rows_at_once = 16

    def step(index, carry):
        rows = pl.ds(pl.multiple_of(index * rows_at_once, rows_at_once), rows_at_once)
        values = [
            (load(part, 0, rows).astype(F32), load(part, 1, rows).astype(F32))
            for part in range(PARTS)
        ]
        for u, (real, imag) in enumerate(eight_point(values)):
            if u:
                cosine, sine = turn_ref[u : u + 1, :], turn_ref[PARTS + u : PARTS + u + 1, :]
                real, imag = real * cosine - imag * sine, real * sine + imag * cosine
            for side, value in enumerate((real, imag)):
                high = value.astype(BF16)
                wh_ref[u, rows, side * COLS : (side + 1) * COLS] = high
                wl_ref[u, rows, side * COLS : (side + 1) * COLS] = (value - high.astype(F32)).astype(BF16)
        return carry

    lax.fori_loop(0, 128 // rows_at_once, step, 0)


def bins_to_features(dh_ref, dl_ref, wh_ref, wl_ref, feat_ref):
    lower_rows = N2 // 2
    for side in range(2):
        feat_ref[side, 0:HALO, :] = jnp.zeros((HALO, 128), F32)
        feat_ref[side, HALO + lower_rows :, :] = jnp.zeros((HALO, 128), F32)
    for pair in range(4):
        wh = wh_ref[2 * pair : 2 * pair + 2].reshape(256, 2 * COLS)
        wl = wl_ref[2 * pair : 2 * pair + 2].reshape(256, 2 * COLS)
        out = three_pass(dh_ref[...], dl_ref[...], wh, wl, ((1,), (1,)))
        power = out[:256] * out[:256] + out[256:] * out[256:]
        feature = jnp.log1p(power * np.float32(1.0 / TOTAL))
        for k in range(2):
            u = 2 * pair + k
            lanes = slice(128 * k, 128 * k + 128)
            feat_ref[0, pl.ds(HALO + u, 128, stride=8), :] = feature[:128, lanes]
            feat_ref[1, pl.ds(HALO + 7 - u, 128, stride=8), :] = feature[128:, lanes]


def second_kernel(x_ref, dh_ref, dl_ref, turn_ref, out_ref, wh_ref, wl_ref, feat_ref):
    combine_columns(lambda part, side, rows: x_ref[part, side, rows, :], turn_ref, wh_ref, wl_ref)
    bins_to_features(dh_ref, dl_ref, wh_ref, wl_ref, feat_ref)
    row = lax.broadcasted_iota(jnp.int32, (128, 128), 0)
    col = lax.broadcasted_iota(jnp.int32, (128, 128), 1)
    mirror = jnp.where(row + col == 127, 1.0, 0.0).astype(BF16)
    for target in range(PARTS):
        rows = pl.ds(target * 128, BLOCK_ROWS)
        out_ref[target, 0] = feat_ref[0, rows, :].astype(BF16)
        out_ref[target, 1] = jnp.dot(
            feat_ref[1, rows, :].astype(BF16), mirror, preferred_element_type=F32
        ).astype(BF16)


def second_section(exchanged):
    table_high, table_low, turn = second_tables()
    return pl.pallas_call(
        second_kernel,
        out_shape=jax.ShapeDtypeStruct((PARTS, 2, BLOCK_ROWS, 128), BF16),
        scratch_shapes=[
            pltpu.VMEM((PARTS, 128, 2 * COLS), BF16),
            pltpu.VMEM((PARTS, 128, 2 * COLS), BF16),
            pltpu.VMEM((2, N2 // 2 + 2 * HALO, 128), F32),
        ],
        name="second_section",
    )(exchanged, jnp.asarray(table_high), jnp.asarray(table_low), jnp.asarray(turn))


def group_mask(channels):
    row_group = lax.broadcasted_iota(jnp.int32, (channels, channels), 0) // GROUP_WIDTH
    col_group = lax.broadcasted_iota(jnp.int32, (channels, channels), 1) // GROUP_WIDTH
    return row_group == col_group


def dense_taps(tap_weights):
    channels = tap_weights.shape[-1]
    tiled = jnp.tile(tap_weights, (1, channels // GROUP_WIDTH, 1))
    return jnp.where(group_mask(channels)[None], tiled, jnp.zeros_like(tiled))


def matmul(a, b, dims):
    return lax.dot_general(a, b, (dims, ((), ())), preferred_element_type=F32)


def local(records, stem_weight, conv_weight, mix_weight, head_weight, labels, band_bounds):
    place = lax.axis_index("freq")
    exchanged = lax.all_to_all(first_section(records[0]), "freq", 0, 0, tiled=True)
    blocks = lax.all_to_all(second_section(exchanged), "freq", 0, 0, tiled=True)
    own_len = TOTAL // 2 // POOL // PARTS
    length = own_len + 16
    blocks = blocks.reshape(4, 2, 2, BLOCK_ROWS, 128)[:, :, :, HALO - 1 : HALO + 129]
    ordered = jnp.concatenate([blocks[:, :, 0], blocks[::-1, :, 1]], axis=0)
    positions = ordered.transpose(2, 0, 1, 3).reshape(length, 256)
    own = slice(8, 8 + own_len)
    q = place * own_len - 8 + lax.broadcasted_iota(jnp.int32, (length, 1), 0)
    valid = (q >= 0) & (q < own_len * PARTS)
    channels = stem_weight.shape[1]
    groups = channels // GROUP_WIDTH
    layers = conv_weight.shape[0]
    stream = matmul(positions, stem_weight, ((1,), (0,)))
    saved = []
    for layer in range(layers):
        dense = dense_taps(conv_weight[layer])
        scale = lax.rsqrt(jnp.mean(stream * stream, axis=-1, keepdims=True) + EPS)
        normed = jnp.where(valid, stream * scale, 0.0).astype(BF16)
        padded = jnp.pad(normed, ((1, 1), (0, 0)))
        preact = sum(matmul(padded[t : t + length], dense[t], ((1,), (0,))) for t in range(KW))
        activated = jax.nn.silu(preact).astype(BF16)
        saved.append((stream, scale, padded, preact, activated, dense))
        stream = stream + matmul(activated, mix_weight[layer], ((1,), (0,)))
    low = jnp.repeat(band_bounds[:-1], GROUP_WIDTH)[None]
    high = jnp.repeat(band_bounds[1:], GROUP_WIDTH)[None]
    counts = ((high - low) // POOL).astype(F32)
    member = (q * POOL >= low) & (q * POOL < high)
    partial_sum = jnp.sum(jnp.where(member, stream, 0.0)[own], axis=0, keepdims=True)
    gathered = lax.all_to_all(
        jnp.broadcast_to(partial_sum[None], (PARTS, 8, channels)), "freq", 0, 0, tiled=True
    )
    pooled = jnp.sum(gathered, axis=0)[:1] / counts
    logits = jnp.dot(pooled, head_weight, precision=EXACT_DOTS)
    exponents = jnp.exp(logits)
    denominator = jnp.sum(exponents, axis=-1, keepdims=True)
    classes = head_weight.shape[1]
    one_hot = (labels[:, None] == lax.broadcasted_iota(jnp.int32, (1, classes), 1)).astype(F32)
    all_records = lax.axis_size("dp")
    lead = (place == 0).astype(F32)
    loss = (jnp.log(denominator[0, 0]) - jnp.sum(one_hot * logits)) / all_records * lead
    grad_logits = (exponents / denominator - one_hot) / all_records
    head_part = grad_logits.T * pooled * lead
    grad_band = jnp.dot(grad_logits, head_weight.T, precision=EXACT_DOTS) / counts
    grad_stream = jnp.where(member, grad_band, 0.0)
    conv_grads, mix_grads = [None] * layers, [None] * layers
    group_row = lax.broadcasted_iota(jnp.int32, (groups, GROUP_WIDTH, channels), 0)
    group_col = lax.broadcasted_iota(jnp.int32, (groups, GROUP_WIDTH, channels), 2) // GROUP_WIDTH
    for layer in reversed(range(layers)):
        stream_in, scale, padded, preact, activated, dense = saved[layer]
        grad_out = grad_stream.astype(BF16)
        mix_grads[layer] = matmul(activated[own], grad_out[own], ((0,), (0,)))
        grad_act = matmul(grad_out, mix_weight[layer], ((1,), (1,)))
        gate = jax.nn.sigmoid(preact)
        grad_pre = grad_act * gate * (1.0 + preact * (1.0 - gate))
        grad_pre = jnp.where(valid, grad_pre, 0.0).astype(BF16)
        own_pre = grad_pre[own]
        taps = []
        for t in range(KW):
            full = matmul(padded[8 + t : 8 + t + own_len], own_pre, ((0,), (0,)))
            full = full.reshape(groups, GROUP_WIDTH, channels)
            taps.append(jnp.sum(jnp.where(group_row == group_col, full, 0.0), axis=0))
        conv_grads[layer] = jnp.concatenate(taps, axis=0)
        grad_padded = jnp.pad(grad_pre, ((1, 1), (0, 0)))
        grad_normed = sum(
            matmul(grad_padded[2 - t : 2 - t + length], dense[t], ((1,), (1,))) for t in range(KW)
        )
        grad_stream = (
            grad_stream
            + scale * grad_normed
            - stream_in * scale**3 * jnp.mean(stream_in * grad_normed, axis=-1, keepdims=True)
        )
    rounded = lax.reduce_precision(grad_stream, 8, 7)
    grad_high = rounded.astype(BF16)
    grad_low = (grad_stream - rounded).astype(BF16)
    own_positions = positions[own]
    grad_stem = matmul(own_positions, grad_high[own], ((0,), (0,))) + matmul(
        own_positions, grad_low[own], ((0,), (0,))
    )
    pieces = [grad_stem] + conv_grads + mix_grads + [
        jnp.pad(head_part, ((0, 16 - classes), (0, 0))).at[15, 0].set(loss)
    ]
    packed = lax.psum(jnp.concatenate(pieces, axis=0), ("dp", "freq"))
    stem_rows = positions.shape[1]
    conv_rows = stem_rows + layers * KW * GROUP_WIDTH
    mix_rows = conv_rows + layers * channels
    return (
        packed[mix_rows + 15, 0],
        packed[:stem_rows],
        packed[stem_rows:conv_rows].reshape(layers, KW, GROUP_WIDTH, channels),
        packed[conv_rows:mix_rows].reshape(layers, channels, channels),
        packed[mix_rows : mix_rows + classes].T,
    )


def solution(mesh):
    in_specs = (P("dp", None, None, "freq"), P(), P(), P(), P(), P("dp"), P())
    out_specs = (P(), P(), P(), P(), P())
    return jax.shard_map(local, mesh=mesh, in_specs=in_specs, out_specs=out_specs, check_vma=False)
```

```python
import functools

import jax
import jax.numpy as jnp
import numpy as np
from jax import lax
from jax.experimental import pallas as pl
from jax.experimental.pallas import tpu as pltpu
from jax.sharding import PartitionSpec as P

EXACT_DOTS = lax.Precision.HIGHEST
EPS = 1e-05
N1 = 1024
N2 = 2048
TOTAL = N1 * N2
POOL = 128
GROUP_WIDTH = 16
KW = 3
PARTS = 8
COLS = N2 // PARTS
HALO = 8
BLOCK_ROWS = N2 // 2 // PARTS + 2 * HALO
BF16 = jnp.bfloat16
F32 = jnp.float32


def split_host(values):
    high = np.asarray(values, np.float32).astype(jnp.bfloat16)
    low = (values - high.astype(np.float64)).astype(jnp.bfloat16)
    return high, low


def first_tables():
    rows = np.arange(N1 // 2, dtype=np.int64)[:, None]
    samples = np.arange(N1 // 2, dtype=np.int64)[None]
    angles = -np.pi * (samples * (2 * rows + 1) % (2 * N1)) / N1
    blocks = [np.cos(angles).reshape(4, 128, -1), np.sin(angles).reshape(4, 128, -1)]
    return split_host(np.stack(blocks, axis=1).reshape(4 * 256, N1 // 2))


def turn_tables():
    rows = np.arange(N1 // 2, dtype=np.int64)[:, None]
    columns = np.arange(COLS, dtype=np.int64)[None]
    angles = -np.pi * (columns * (2 * rows + 1)) / TOTAL
    device_angles = -np.pi * (COLS * np.arange(PARTS, dtype=np.int64)[None] * (2 * rows + 1)) / TOTAL
    shared = np.stack([np.cos(angles), np.sin(angles)]).astype(np.float32)
    own = np.concatenate([np.cos(device_angles), np.sin(device_angles)], axis=1).astype(np.float32)
    return shared, own


def second_tables():
    order = np.concatenate([np.arange(128), np.arange(255, 127, -1)]).astype(np.int64)
    columns = np.arange(COLS, dtype=np.int64)[None]
    angles = -2 * np.pi * (order[:, None] * columns % COLS) / COLS
    cosine, sine = np.cos(angles), np.sin(angles)
    upper = np.concatenate([cosine, -sine], axis=1)
    lower = np.concatenate([sine, cosine], axis=1)
    lanes = -2 * np.pi * (np.arange(PARTS, dtype=np.int64)[:, None] * columns) / N2
    turn = np.concatenate([np.cos(lanes), np.sin(lanes)], axis=0).astype(np.float32)
    return split_host(np.concatenate([upper, lower], axis=0)) + (turn,)


def three_pass(lhs_high, lhs_low, rhs_high, rhs_low, dims):
    product = functools.partial(
        lax.dot_general, dimension_numbers=(dims, ((), ())), preferred_element_type=F32
    )
    return product(lhs_high, rhs_high) + (product(lhs_high, rhs_low) + product(lhs_low, rhs_high))


def first_kernel(x_ref, th_ref, tl_ref, turn_ref, own_ref, out_ref, xh_ref, xl_ref):
    @pl.when(pl.program_id(0) == 0)
    def _():
        for channel in range(2):
            for piece in range(4):
                rows = pl.ds(piece * 256, 256)
                value = x_ref[channel, rows, :]
                high = value.astype(BF16)
                xh_ref[channel, rows, :] = high
                xl_ref[channel, rows, :] = (value - high.astype(F32)).astype(BF16)

    place = lax.axis_index("freq")
    lane = lax.broadcasted_iota(jnp.int32, (128, 2 * PARTS), 1)
    own = own_ref[...]
    own_cos = jnp.sum(jnp.where(lane == place, own, 0.0), axis=1, keepdims=True)
    own_sin = jnp.sum(jnp.where(lane == place + PARTS, own, 0.0), axis=1, keepdims=True)
    cosine = turn_ref[0] * own_cos - turn_ref[1] * own_sin
    sine = turn_ref[0] * own_sin + turn_ref[1] * own_cos
    row = lax.broadcasted_iota(jnp.int32, (128, COLS), 0)
    sign = jnp.where(row % 2 == 0, 1.0, -1.0)
    for channel in range(2):
        parts = []
        for half in range(2):
            rows = pl.ds(half * 512, 512)
            parts.append(
                three_pass(
                    th_ref[...], tl_ref[...], xh_ref[channel, rows, :], xl_ref[channel, rows, :],
                    ((1,), (0,)),
                )
            )
        real = parts[0][:128] + sign * parts[1][128:]
        imag = parts[0][128:] - sign * parts[1][:128]
        out_ref[channel, 0] = real * cosine - imag * sine
        out_ref[channel, 1] = real * sine + imag * cosine


def first_section(records):
    table_high, table_low = first_tables()
    shared, own = turn_tables()
    return pl.pallas_call(
        first_kernel,
        grid=(4,),
        out_shape=jax.ShapeDtypeStruct((PARTS, 2, 128, COLS), F32),
        in_specs=[
            pl.BlockSpec((2, N1, COLS), lambda j: (0, 0, 0)),
            pl.BlockSpec((256, 512), lambda j: (j, 0)),
            pl.BlockSpec((256, 512), lambda j: (j, 0)),
            pl.BlockSpec((2, 128, COLS), lambda j: (0, j, 0)),
            pl.BlockSpec((128, 2 * PARTS), lambda j: (j, 0)),
        ],
        out_specs=pl.BlockSpec((2, 2, 128, COLS), lambda j: (j, 0, 0, 0)),
        scratch_shapes=[pltpu.VMEM((2, N1, COLS), BF16)] * 2,
        name="first_section",
    )(records, jnp.asarray(table_high), jnp.asarray(table_low), jnp.asarray(shared), jnp.asarray(own))


def eight_point(values):
    root = np.float32(np.sqrt(0.5))

    def add(a, b):
        return (a[0] + b[0], a[1] + b[1])

    def sub(a, b):
        return (a[0] - b[0], a[1] - b[1])

    def quarter(a):
        return (a[1], -a[0])

    def four(a):
        s02, d02, s13, d13 = add(a[0], a[2]), sub(a[0], a[2]), add(a[1], a[3]), sub(a[1], a[3])
        turned = quarter(d13)
        return [add(s02, s13), add(d02, turned), sub(s02, s13), sub(d02, turned)]

    even, odd = four(values[0::2]), four(values[1::2])
    turned = [
        odd[0],
        ((odd[1][0] + odd[1][1]) * root, (odd[1][1] - odd[1][0]) * root),
        quarter(odd[2]),
        ((odd[3][1] - odd[3][0]) * root, -(odd[3][0] + odd[3][1]) * root),
    ]
    return [add(even[i], turned[i]) for i in range(4)] + [sub(even[i], turned[i]) for i in range(4)]


def combine_columns(load, turn_ref, wh_ref, wl_ref):
    rows_at_once = 16

    def step(index, carry):
        rows = pl.ds(pl.multiple_of(index * rows_at_once, rows_at_once), rows_at_once)
        values = [
            (load(part, 0, rows), load(part, 1, rows))
            for part in range(PARTS)
        ]
        for u, (real, imag) in enumerate(eight_point(values)):
            if u:
                cosine, sine = turn_ref[u : u + 1, :], turn_ref[PARTS + u : PARTS + u + 1, :]
                real, imag = real * cosine - imag * sine, real * sine + imag * cosine
            for side, value in enumerate((real, imag)):
                high = value.astype(BF16)
                wh_ref[u, rows, side * COLS : (side + 1) * COLS] = high
                wl_ref[u, rows, side * COLS : (side + 1) * COLS] = (value - high.astype(F32)).astype(BF16)
        return carry

    lax.fori_loop(0, 128 // rows_at_once, step, 0)


def bins_to_features(dh_ref, dl_ref, wh_ref, wl_ref, feat_ref):
    lower_rows = N2 // 2
    for side in range(2):
        feat_ref[side, 0:HALO, :] = jnp.zeros((HALO, 128), F32)
        feat_ref[side, HALO + lower_rows :, :] = jnp.zeros((HALO, 128), F32)
    for pair in range(4):
        wh = wh_ref[2 * pair : 2 * pair + 2].reshape(256, 2 * COLS)
        wl = wl_ref[2 * pair : 2 * pair + 2].reshape(256, 2 * COLS)
        out = three_pass(dh_ref[...], dl_ref[...], wh, wl, ((1,), (1,)))
        power = out[:256] * out[:256] + out[256:] * out[256:]
        feature = jnp.log1p(power * np.float32(1.0 / TOTAL))
        for k in range(2):
            u = 2 * pair + k
            lanes = slice(128 * k, 128 * k + 128)
            feat_ref[0, pl.ds(HALO + u, 128, stride=8), :] = feature[:128, lanes]
            feat_ref[1, pl.ds(HALO + 7 - u, 128, stride=8), :] = feature[128:, lanes]


def second_kernel(x_ref, dh_ref, dl_ref, turn_ref, out_ref, wh_ref, wl_ref, feat_ref):
    combine_columns(lambda part, side, rows: x_ref[part, side, rows, :], turn_ref, wh_ref, wl_ref)
    bins_to_features(dh_ref, dl_ref, wh_ref, wl_ref, feat_ref)
    row = lax.broadcasted_iota(jnp.int32, (128, 128), 0)
    col = lax.broadcasted_iota(jnp.int32, (128, 128), 1)
    mirror = jnp.where(row + col == 127, 1.0, 0.0).astype(BF16)
    for target in range(PARTS):
        rows = pl.ds(target * 128, BLOCK_ROWS)
        out_ref[target, 0] = feat_ref[0, rows, :].astype(BF16)
        out_ref[target, 1] = jnp.dot(
            feat_ref[1, rows, :].astype(BF16), mirror, preferred_element_type=F32
        ).astype(BF16)


def second_section(exchanged):
    table_high, table_low, turn = second_tables()
    return pl.pallas_call(
        second_kernel,
        out_shape=jax.ShapeDtypeStruct((PARTS, 2, BLOCK_ROWS, 128), BF16),
        scratch_shapes=[
            pltpu.VMEM((PARTS, 128, 2 * COLS), BF16),
            pltpu.VMEM((PARTS, 128, 2 * COLS), BF16),
            pltpu.VMEM((2, N2 // 2 + 2 * HALO, 128), F32),
        ],
        name="second_section",
    )(exchanged, jnp.asarray(table_high), jnp.asarray(table_low), jnp.asarray(turn))


MESH = pl.DeviceIdType.MESH
SIDE = 4
PART_ROWS = (1536, 1536, 512)
PART_LANES = (128, 128, 256)
PART_AXES = ((0, 1, 2), (1, 2, 0), (2, 0, 1))
STEM_ROWS, CONV_ROWS, REST_ROWS = 256, 144, 16


def reduce_kernel(
    mix_ref, stem_ref, conv_ref, rest_ref, mix_out, stem_out, conv_out, rest_out, *scratch
):
    acc = scratch[0:3]
    pair = scratch[3:6]
    full = scratch[6:9]
    landing = [scratch[9 + 3 * part : 12 + 3 * part] for part in range(3)]
    pair_send, pair_recv, send, recv = scratch[18:22]
    dp, freq = lax.axis_index("dp"), lax.axis_index("freq")
    core = dp % 2
    spot = (freq // 2, dp // 4, (freq % 2) * 2 + (dp // 2) % 2)

    def device(place, which):
        x, y, z = place
        return {"dp": (y * 2 + z % 2) * 2 + which, "freq": x * 2 + z // 2}

    def neighbour(axis, distance):
        place = list(spot)
        place[axis] = (spot[axis] + distance) % SIDE
        return device(place, core), place[axis]

    partner = device(spot, 1 - core)
    barrier = pltpu.get_barrier_semaphore()
    pl.semaphore_signal(barrier, inc=1, device_id=partner, device_id_type=MESH)
    for axis in range(3):
        for distance in range(1, SIDE):
            pl.semaphore_signal(
                barrier, inc=1, device_id=neighbour(axis, distance)[0], device_id_type=MESH
            )
    pl.semaphore_wait(barrier, 10)

    def lanes(owner, start, size):
        return pl.ds(pl.multiple_of(owner * 256 + start, 128), size)

    def pieces(mix, stem, conv, rest):
        first = STEM_ROWS + CONV_ROWS
        return (
            (0, mix, 0, 128, slice(0, 1536)),
            (1, mix, 128, 128, slice(0, 1536)),
            (2, stem, 0, 256, slice(0, STEM_ROWS)),
            (2, conv, 0, 256, slice(STEM_ROWS, first)),
            (2, rest, 0, 256, slice(first, first + REST_ROWS)),
        )

    inputs = pieces(mix_ref, stem_ref, conv_ref, rest_ref)
    outputs = pieces(mix_out, stem_out, conv_out, rest_out)
    copies = []
    for index, (part, ref, start, size, rows) in enumerate(inputs):
        copies.append(
            pltpu.make_async_remote_copy(
                src_ref=ref.at[:, lanes(1 - core, start, size)],
                dst_ref=pair[part].at[rows, :],
                send_sem=pair_send.at[0, index],
                recv_sem=pair_recv.at[0, index],
                device_id=partner,
                device_id_type=MESH,
            )
        )
        copies[-1].start()
    used = STEM_ROWS + CONV_ROWS + REST_ROWS
    acc[2][used:, :] = jnp.zeros((PART_ROWS[2] - used, PART_LANES[2]), F32)

    counts = [[rows // SIDE ** (stage + 1) for stage in range(3)] for rows in PART_ROWS]
    offsets = []
    for part in range(3):
        chain = [0]
        for stage in range(3):
            chain.append(chain[-1] + spot[PART_AXES[part][stage]] * counts[part][stage])
        offsets.append(chain)

    def window(part, start, stage):
        return pl.ds(pl.multiple_of(start, 8), counts[part][stage])

    def scatter(part, stage):
        started = []
        for distance in range(1, SIDE):
            target, coordinate = neighbour(PART_AXES[part][stage], distance)
            start = offsets[part][stage] + coordinate * counts[part][stage]
            started.append(
                pltpu.make_async_remote_copy(
                    src_ref=acc[part].at[window(part, start, stage), :],
                    dst_ref=landing[part][stage].at[distance - 1],
                    send_sem=send.at[part, stage, distance - 1],
                    recv_sem=recv.at[part, stage, distance - 1],
                    device_id=target,
                    device_id_type=MESH,
                )
            )
            started[-1].start()
        return started

    def gather(part, stage):
        started = []
        rows = window(part, offsets[part][stage + 1], stage)
        for distance in range(1, SIDE):
            target, _ = neighbour(PART_AXES[part][stage], distance)
            started.append(
                pltpu.make_async_remote_copy(
                    src_ref=full[part].at[rows, :],
                    dst_ref=full[part].at[rows, :],
                    send_sem=send.at[part, 3 + stage, distance - 1],
                    recv_sem=recv.at[part, 3 + stage, distance - 1],
                    device_id=target,
                    device_id_type=MESH,
                )
            )
            started[-1].start()
        return started

    flying = [None] * 3
    for index, (part, ref, start, size, rows) in enumerate(inputs):
        copies[index].wait()
        acc[part][rows, :] = ref[:, lanes(core, start, size)] + pair[part][rows, :]
        if index != 2 and index != 3:
            flying[part] = scatter(part, 0)
    for stage in range(3):
        for part in range(3):
            for copy in flying[part]:
                copy.wait()
            rows = window(part, offsets[part][stage + 1], stage)
            arrived = landing[part][stage]
            total = acc if stage < 2 else full
            total[part][rows, :] = (acc[part][rows, :] + arrived[0]) + (arrived[1] + arrived[2])
            flying[part] = scatter(part, stage + 1) if stage < 2 else gather(part, 2)
    for stage in (1, 0):
        for part in range(3):
            for copy in flying[part]:
                copy.wait()
            flying[part] = gather(part, stage)
    last = []
    for index, (part, ref, start, size, rows) in enumerate(outputs):
        if index < 3:
            for copy in flying[part]:
                copy.wait()
        last.append(
            pltpu.make_async_remote_copy(
                src_ref=full[part].at[rows, :],
                dst_ref=ref.at[:, lanes(core, start, size)],
                send_sem=pair_send.at[1, index],
                recv_sem=pair_recv.at[1, index],
                device_id=partner,
                device_id_type=MESH,
            )
        )
        last[-1].start()
        ref[:, lanes(core, start, size)] = full[part][rows, :]
    for copy in last:
        copy.wait()


def reduce_everywhere(mix, stem, conv, rest):
    buffers = [pltpu.VMEM((rows, width), F32) for rows, width in zip(PART_ROWS, PART_LANES)]
    landing = [
        pltpu.VMEM((SIDE - 1, rows // SIDE ** (stage + 1), width), F32)
        for rows, width in zip(PART_ROWS, PART_LANES)
        for stage in range(3)
    ]
    arrays = (mix, stem, conv, rest)
    return pl.pallas_call(
        reduce_kernel,
        out_shape=[jax.ShapeDtypeStruct(a.shape, F32) for a in arrays],
        in_specs=[pl.BlockSpec(memory_space=pltpu.VMEM)] * 4,
        out_specs=[pl.BlockSpec(memory_space=pltpu.VMEM)] * 4,
        scratch_shapes=buffers
        + buffers
        + buffers
        + landing
        + [pltpu.SemaphoreType.DMA((2, 5))] * 2
        + [pltpu.SemaphoreType.DMA((3, 6, 3))] * 2,
        compiler_params=pltpu.CompilerParams(collective_id=0, has_side_effects=True),
        name="reduce_everywhere",
    )(*arrays)


def group_mask(channels):
    row_group = lax.broadcasted_iota(jnp.int32, (channels, channels), 0) // GROUP_WIDTH
    col_group = lax.broadcasted_iota(jnp.int32, (channels, channels), 1) // GROUP_WIDTH
    return row_group == col_group


def dense_taps(tap_weights):
    channels = tap_weights.shape[-1]
    tiled = jnp.tile(tap_weights, (1, channels // GROUP_WIDTH, 1))
    return jnp.where(group_mask(channels)[None], tiled, jnp.zeros_like(tiled))


def matmul(a, b, dims):
    return lax.dot_general(a, b, (dims, ((), ())), preferred_element_type=F32)


def local(records, stem_weight, conv_weight, mix_weight, head_weight, labels, band_bounds):
    place = lax.axis_index("freq")
    exchanged = lax.all_to_all(first_section(records[0]), "freq", 0, 0, tiled=True)
    blocks = lax.all_to_all(second_section(exchanged), "freq", 0, 0, tiled=True)
    own_len = TOTAL // 2 // POOL // PARTS
    length = own_len + 16
    blocks = blocks.reshape(4, 2, 2, BLOCK_ROWS, 128)[:, :, :, HALO - 1 : HALO + 129]
    ordered = jnp.concatenate([blocks[:, :, 0], blocks[::-1, :, 1]], axis=0)
    positions = ordered.transpose(2, 0, 1, 3).reshape(length, 256)
    own = slice(8, 8 + own_len)
    q = place * own_len - 8 + lax.broadcasted_iota(jnp.int32, (length, 1), 0)
    valid = (q >= 0) & (q < own_len * PARTS)
    channels = stem_weight.shape[1]
    groups = channels // GROUP_WIDTH
    layers = conv_weight.shape[0]
    stream = matmul(positions, stem_weight, ((1,), (0,)))
    saved = []
    for layer in range(layers):
        dense = dense_taps(conv_weight[layer])
        scale = lax.rsqrt(jnp.mean(stream * stream, axis=-1, keepdims=True) + EPS)
        normed = jnp.where(valid, stream * scale, 0.0).astype(BF16)
        padded = jnp.pad(normed, ((1, 1), (0, 0)))
        preact = sum(matmul(padded[t : t + length], dense[t], ((1,), (0,))) for t in range(KW))
        activated = jax.nn.silu(preact).astype(BF16)
        saved.append((stream, scale, padded, preact, activated, dense))
        stream = stream + matmul(activated, mix_weight[layer], ((1,), (0,)))
    low = jnp.repeat(band_bounds[:-1], GROUP_WIDTH)[None]
    high = jnp.repeat(band_bounds[1:], GROUP_WIDTH)[None]
    counts = ((high - low) // POOL).astype(F32)
    member = (q * POOL >= low) & (q * POOL < high)
    partial_sum = jnp.sum(jnp.where(member, stream, 0.0)[own], axis=0, keepdims=True)
    gathered = lax.all_to_all(
        jnp.broadcast_to(partial_sum[None], (PARTS, 8, channels)), "freq", 0, 0, tiled=True
    )
    pooled = jnp.sum(gathered, axis=0)[:1] / counts
    logits = jnp.dot(pooled, head_weight, precision=EXACT_DOTS)
    exponents = jnp.exp(logits)
    denominator = jnp.sum(exponents, axis=-1, keepdims=True)
    classes = head_weight.shape[1]
    one_hot = (labels[:, None] == lax.broadcasted_iota(jnp.int32, (1, classes), 1)).astype(F32)
    all_records = lax.axis_size("dp")
    lead = (place == 0).astype(F32)
    loss = (jnp.log(denominator[0, 0]) - jnp.sum(one_hot * logits)) / all_records * lead
    grad_logits = (exponents / denominator - one_hot) / all_records
    head_part = grad_logits.T * pooled * lead
    grad_band = jnp.dot(grad_logits, head_weight.T, precision=EXACT_DOTS) / counts
    grad_stream = jnp.where(member, grad_band, 0.0)
    conv_grads, mix_grads = [None] * layers, [None] * layers
    group_row = lax.broadcasted_iota(jnp.int32, (groups, GROUP_WIDTH, channels), 0)
    group_col = lax.broadcasted_iota(jnp.int32, (groups, GROUP_WIDTH, channels), 2) // GROUP_WIDTH
    for layer in reversed(range(layers)):
        stream_in, scale, padded, preact, activated, dense = saved[layer]
        grad_out = grad_stream.astype(BF16)
        mix_grads[layer] = matmul(activated[own], grad_out[own], ((0,), (0,)))
        grad_act = matmul(grad_out, mix_weight[layer], ((1,), (1,)))
        gate = jax.nn.sigmoid(preact)
        grad_pre = grad_act * gate * (1.0 + preact * (1.0 - gate))
        grad_pre = jnp.where(valid, grad_pre, 0.0).astype(BF16)
        own_pre = grad_pre[own]
        taps = []
        for t in range(KW):
            full = matmul(padded[8 + t : 8 + t + own_len], own_pre, ((0,), (0,)))
            full = full.reshape(groups, GROUP_WIDTH, channels)
            taps.append(jnp.sum(jnp.where(group_row == group_col, full, 0.0), axis=0))
        conv_grads[layer] = jnp.concatenate(taps, axis=0)
        grad_padded = jnp.pad(grad_pre, ((1, 1), (0, 0)))
        grad_normed = sum(
            matmul(grad_padded[2 - t : 2 - t + length], dense[t], ((1,), (1,))) for t in range(KW)
        )
        grad_stream = (
            grad_stream
            + scale * grad_normed
            - stream_in * scale**3 * jnp.mean(stream_in * grad_normed, axis=-1, keepdims=True)
        )
    rounded = lax.reduce_precision(grad_stream, 8, 7)
    grad_high = rounded.astype(BF16)
    grad_low = (grad_stream - rounded).astype(BF16)
    own_positions = positions[own]
    grad_stem = matmul(own_positions, grad_high[own], ((0,), (0,))) + matmul(
        own_positions, grad_low[own], ((0,), (0,))
    )
    rest = jnp.pad(head_part, ((0, REST_ROWS - classes), (0, 0))).at[REST_ROWS - 1, 0].set(loss)
    mix_all, stem_all, conv_all, rest_all = reduce_everywhere(
        jnp.concatenate(mix_grads, axis=0), grad_stem, jnp.concatenate(conv_grads, axis=0), rest
    )
    return (
        rest_all[REST_ROWS - 1, 0],
        stem_all,
        conv_all.reshape(layers, KW, GROUP_WIDTH, channels),
        mix_all.reshape(layers, channels, channels),
        rest_all[:classes].T,
    )


def solution(mesh):
    in_specs = (P("dp", None, None, "freq"), P(), P(), P(), P(), P("dp"), P())
    out_specs = (P(), P(), P(), P(), P())
    return jax.shard_map(local, mesh=mesh, in_specs=in_specs, out_specs=out_specs, check_vma=False)
```
